32 devices in a mesh: pipe: 4 (over z), ctx: 8 (over y, x, core).
Axes of the slice: x: 2, y: 2, z: 4, core: 2. Of those that a mesh axis runs over, the one named last changes fastest.
Arguments:
- queries: bfloat16 [4, 2048, 4096], P('pipe', 'ctx'), may hold values from -110 to 110
- keys: bfloat16 [4, 2048, 512], P('pipe', 'ctx'), may hold values from -4 to 4
- values: bfloat16 [4, 2048, 512], P('pipe', 'ctx'), may hold values from -6 to 6
- doc_ids: int32 [4, 8], P('pipe'), may hold values from 0 to 1, never falling along the last dimension, each value on 1 to 5 neighbouring positions
Outputs:
- handed: bfloat16 [4, 2048, 4096], P('pipe', 'ctx')
The draws below stay inside these ranges and needn't reach their ends.
Inputs may be any that keep to these rules, and one draw needn't show every extreme that they name: doc_ids never falls along a section's blocks; each document spans 1 to 5 blocks.
All inputs are finite; a program needn't handle non-finite values.
Results may differ from the reference program's by a relative error of at most 0.004.
Values may be sent and summed in bfloat16 or wider, within the bound.
A program may use at most 320 MiB of HBM per device.

```python
import math
import jax
import jax.numpy as jnp
import numpy as np
from jax import lax

HQ = 32
HK = 4
DH = 128
TOK_DEV = 256
SECTIONS = 4
SEQ = 2048
DOC_MOST = 5
DOC_COUNT = 2
N_CTX = 8


def key_field(key):
    field = jax.random.normal(jax.random.fold_in(key, 11), (SECTIONS, SEQ, HK * DH), jnp.float32)
    return jnp.clip(field, -4.0, 4.0)


def draw_keys(key, part):
    field = key_field(key)
    return field.astype(jnp.bfloat16)


def draw_queries(key, part):
    field = jax.random.normal(jax.random.fold_in(key, 23), (SECTIONS, SEQ, HQ * DH), jnp.float32)
    field = jnp.clip(field, -4.0, 4.0)
    return field.astype(jnp.bfloat16)


def block_scale(own_key, extent, split, smallest, top_value):
    factor_of = 1.0
    for axis_at, blocks in split:
        draws = jax.random.uniform(jax.random.fold_in(jax.random.fold_in(own_key, 6), axis_at), (blocks,), jnp.float32, smallest / len(split), top_value / len(split))
        factor_of = factor_of * jnp.repeat(jnp.exp(draws), extent[axis_at] // blocks).reshape((-1,) + (1,) * (len(extent) - 1 - axis_at))
    return factor_of


def profile(number_of, total, reach, skew):
    loads = [(1 << 20) // math.isqrt(grade ** skew) + 1 for grade in range(2, number_of + 1)]
    spare, given = total - reach - (number_of - 1), [1] * (number_of - 1)
    while spare > 0:
        candidates = [i for i in range(number_of - 1) if given[i] < reach]
        mass, budget = sum([loads[i] for i in candidates]), spare
        for i in candidates:
            more = min(reach - given[i], max(1, budget * loads[i] // mass), spare)
            given[i] = given[i] + more
            spare = spare - more
    return np.array([reach] + given)


def uneven(own_key, count, total, reach, slope):
    if count == 2:
        one = jax.random.randint(own_key, (), max(1, total - reach), min(reach, total - 1) + 1)
        return jnp.stack([one, total - one])
    tallies = jnp.asarray(profile(count, total, reach, slope), jnp.int32)
    couples = (count - 1) // 2
    giver, sink = tallies[1:1 + 2 * couples:2], tallies[2:2 + 2 * couples:2]
    room = jnp.minimum(giver - 1, reach - sink)
    shifted = jax.random.randint(jax.random.fold_in(own_key, 1), (couples,), 0, 1 << 20) % (room + 1)
    tallies = tallies.at[1:1 + 2 * couples:2].set(giver - shifted).at[2:2 + 2 * couples:2].set(sink + shifted)
    return tallies[jax.random.permutation(jax.random.fold_in(own_key, 2), count)]


def bell_draw(key, shape, width, most, pieces=(), held_as=jnp.bfloat16):
    gain = block_scale(key, shape, pieces, -0.22, 0.18) if pieces else 1.0
    values = jax.random.normal(key, shape, jnp.float32) * width * gain
    return jnp.minimum(jnp.maximum(values, -most), most).astype(held_as)


def setup_inputs(seed: int = 0) -> dict:
    key_list = jax.random.split(jax.random.key(seed), 5)
    return {
        "queries": draw_queries(jax.random.fold_in(key_list[4], 71), 0),
        "keys": draw_keys(jax.random.fold_in(key_list[4], 71), 0),
        "values": bell_draw(key_list[2], (SECTIONS, SEQ, HK * DH), 1.0, 6.0, ((0, 4), (1, 8))),
        "doc_ids": jax.vmap(lambda own: jnp.searchsorted(jnp.cumsum(uneven(own, DOC_COUNT, N_CTX, DOC_MOST, 0)), jnp.arange(N_CTX), side="right"))(jax.random.split(key_list[3], SECTIONS)).reshape((SECTIONS, N_CTX)).astype(jnp.int32),
    }


def reference(queries, keys, values, doc_ids):
    per_group = HQ // HK
    score_scale = 1.0 / math.sqrt(DH)

    def one_section(section_in):
        q_sec, k_sec, v_sec, doc_row = section_in
        key_heads = k_sec.astype(jnp.float32).reshape(SEQ, HK, DH)
        value_heads = v_sec.astype(jnp.float32).reshape(SEQ, HK, DH)
        key_pos = jnp.arange(SEQ, dtype=jnp.int32)
        key_doc = doc_row[(key_pos // TOK_DEV).astype(jnp.int32)]
        q_blocks = q_sec.reshape(N_CTX, TOK_DEV, HK, per_group, DH)

        def one_block(block_in):
            q_blk, blk_index = block_in
            query_pos = blk_index * TOK_DEV + jnp.arange(TOK_DEV, dtype=jnp.int32)
            scores = jnp.einsum('qhgd,khd->hgqk', q_blk.astype(jnp.float32), key_heads) * score_scale
            own_doc = doc_row[blk_index]
            visible = (key_doc[None, :] == own_doc) & (key_pos[None, :] <= query_pos[:, None])
            masked = jnp.where(visible, scores, -1e+30)
            row_top = lax.optimization_barrier(jnp.max(masked, axis=-1, keepdims=True))
            weights = jnp.where(visible, jnp.exp(masked - row_top), 0.0)
            row_total = lax.optimization_barrier(jnp.sum(weights, axis=-1, keepdims=True))
            rounded = lax.optimization_barrier(weights.astype(jnp.bfloat16))
            summed = jnp.einsum('hgqk,khd->hgqd', rounded.astype(jnp.float32), value_heads)
            attended = summed / row_total
            return attended.transpose(2, 0, 1, 3).reshape(TOK_DEV, HQ * DH).astype(jnp.bfloat16)
        blocks_out = lax.map(one_block, (q_blocks, jnp.arange(N_CTX, dtype=jnp.int32)))
        return blocks_out.reshape(SEQ, HQ * DH)
    attended_all = lax.map(one_section, (queries, keys, values, doc_ids))
    return jnp.roll(attended_all, 1, axis=0)
```

```python
import functools
import math

import jax
import jax.numpy as jnp
from jax import lax
from jax.experimental import pallas as pl
from jax.experimental.pallas import tpu as pltpu
from jax.sharding import PartitionSpec as P

HQ = 32
HK = 4
DH = 128
PER_GROUP = HQ // HK
STEP_HEADS = 2
HIDDEN = 1e30
MESH = pl.DeviceIdType.MESH


def kernel(
    n_pipe,
    n_ctx,
    window,
    rows,
    doc_ref,
    q_ref,
    k_ref,
    v_ref,
    out_ref,
    qbuf,
    kbuf,
    vbuf,
    obuf,
    bias,
    q_sem,
    own_sem,
    kv_send,
    kv_recv,
    z_send,
    z_recv,
    o_send,
    o_recv,
):
    pipe = lax.axis_index("pipe")
    ctx = lax.axis_index("ctx")
    right = lax.rem(pipe + 1, n_pipe)
    left = lax.rem(pipe + n_pipe - 1, n_pipe)
    moved = HK - 1
    group_cols = PER_GROUP * DH
    step_cols = STEP_HEADS * DH
    steps = HQ // STEP_HEADS
    group_steps = PER_GROUP // STEP_HEADS
    sent_steps = moved * group_steps
    last = window - 1

    barrier = pltpu.get_barrier_semaphore()
    pl.semaphore_signal(barrier, inc=1, device_id=(left, ctx), device_id_type=MESH)
    pl.semaphore_signal(barrier, inc=1, device_id=(right, ctx), device_id_type=MESH)
    for d in range(1, window):

        @pl.when(ctx >= d)
        def _():
            pl.semaphore_signal(barrier, inc=1, device_id=(pipe, ctx - d), device_id_type=MESH)

        @pl.when(ctx + d < n_ctx)
        def _():
            pl.semaphore_signal(barrier, inc=1, device_id=(pipe, ctx + d), device_id_type=MESH)

    def own_copies(g):
        cols = pl.ds(pl.multiple_of(g * DH, DH), DH)
        place = pl.ds(last * rows, rows)
        return (
            pltpu.make_async_copy(k_ref.at[:, cols], kbuf.at[g, place], own_sem.at[0, g]),
            pltpu.make_async_copy(v_ref.at[:, cols], vbuf.at[g, place], own_sem.at[1, g]),
        )

    def q_copy(g):
        cols = pl.ds(pl.multiple_of(g * group_cols, group_cols), group_cols)
        return pltpu.make_async_copy(q_ref.at[:, cols], qbuf.at[:, cols], q_sem.at[g])

    def gather_copies(g, d):
        source = pl.ds(last * rows, rows)
        place = pl.ds((last - d) * rows, rows)
        return [
            pltpu.make_async_remote_copy(
                src_ref=buf.at[g, source],
                dst_ref=buf.at[g, place],
                send_sem=kv_send.at[which, g, d - 1],
                recv_sem=kv_recv.at[which, g, d - 1],
                device_id=(pipe, lax.rem(ctx + d, n_ctx)),
                device_id_type=MESH,
            )
            for which, buf in ((0, kbuf), (1, vbuf))
        ]

    def to_right(source, target, at):
        return pltpu.make_async_remote_copy(
            src_ref=source,
            dst_ref=target,
            send_sem=z_send.at[at],
            recv_sem=z_recv.at[at],
            device_id=(right, ctx),
            device_id_type=MESH,
        )

    def moved_copies():
        cols = pl.ds(moved * DH, DH)
        q_cols = pl.ds(moved * group_cols, group_cols)
        place = pl.ds(last * rows, rows)
        return (
            to_right(k_ref.at[:, cols], kbuf.at[moved, place], 0),
            to_right(v_ref.at[:, cols], vbuf.at[moved, place], 1),
            to_right(bias.at[0], bias.at[1], 2),
            to_right(q_ref.at[:, q_cols], qbuf.at[:, q_cols], 3),
        )

    def out_copy(step):
        cols = pl.ds(pl.multiple_of(step * step_cols, step_cols), step_cols)
        return pltpu.make_async_remote_copy(
            src_ref=obuf.at[:, cols],
            dst_ref=out_ref.at[:, cols],
            send_sem=o_send.at[step],
            recv_sem=o_recv.at[step],
            device_id=(right, ctx),
            device_id_type=MESH,
        )

    def out_local(step):
        cols = pl.ds(pl.multiple_of(step * step_cols, step_cols), step_cols)
        return pltpu.make_async_copy(obuf.at[:, cols], out_ref.at[:, cols], o_send.at[step])

    for g in range(moved):
        for copy in own_copies(g):
            copy.start()
        q_copy(g).start()

    bias[0] = jnp.zeros(bias.shape[1:], jnp.float32)
    own_doc = doc_ref[0, ctx]
    for d in range(window):
        block = jnp.maximum(ctx - d, 0)
        seen = (doc_ref[0, block] == own_doc) & (ctx >= d)
        bias[0, d : d + 1, :] = jnp.full((1, DH), jnp.where(seen, 0.0, HIDDEN), jnp.float32)

    for d in range(1, window):

        @pl.when(ctx < d)
        def _():
            place = pl.ds((last - d) * rows, rows)
            for g in range(HK):
                kbuf[g, place, :] = jnp.zeros((rows, DH), kbuf.dtype)
                vbuf[g, place, :] = jnp.zeros((rows, DH), vbuf.dtype)

    met = 2
    for d in range(1, window):
        met = met + jnp.where(ctx >= d, 1, 0) + jnp.where(ctx + d < n_ctx, 1, 0)
    pl.semaphore_wait(barrier, met)

    for copy in moved_copies():
        copy.start()

    def start_gather(g):
        @pl.when(g < moved)
        def _():
            for copy in own_copies(g):
                copy.wait()

        @pl.when(g == moved)
        def _():
            for copy in moved_copies()[:3]:
                copy.wait_recv()

        for d in range(1, window):

            @pl.when(ctx + d < n_ctx)
            def _():
                for copy in gather_copies(g, d):
                    copy.start()

    def end_gather(g):
        for d in range(1, window):

            @pl.when(ctx >= d)
            def _():
                for copy in gather_copies(g, d):
                    copy.wait_recv()

    start_gather(0)
    factor = math.log2(math.e) / math.sqrt(DH)

    @pl.loop(0, steps)
    def _(step):
        g = step // group_steps

        @pl.when(lax.rem(step, group_steps) == 0)
        def _():
            @pl.when(g < moved)
            def _():
                q_copy(g).wait()

            @pl.when(g == moved)
            def _():
                moved_copies()[3].wait_recv()

            end_gather(g)

            @pl.when(g < moved)
            def _():
                start_gather(g + 1)

        which = jnp.where(g == moved, 1, 0)
        causal = lax.broadcasted_iota(jnp.int32, (rows, rows), 0) >= lax.broadcasted_iota(
            jnp.int32, (rows, rows), 1
        )
        for at in range(STEP_HEADS):
            cols = pl.ds(pl.multiple_of(step * step_cols + at * DH, DH), DH)
            query = qbuf[:, cols]
            scores = []
            top = None
            for d in range(window):
                place = pl.ds((last - d) * rows, rows)
                part = lax.dot_general(
                    query,
                    kbuf[g, place, :],
                    (((1,), (1,)), ((), ())),
                    preferred_element_type=jnp.float32,
                )
                if d == 0:
                    part = jnp.where(causal, part, -HIDDEN)
                scores.append(part)
                lanes = part[:, :DH]
                for c in range(1, rows // DH):
                    lanes = jnp.maximum(lanes, part[:, c * DH : (c + 1) * DH])
                if d > 0:
                    lanes = lanes - bias[which, d : d + 1, :]
                top = lanes if top is None else jnp.maximum(top, lanes)
            row_top = jnp.max(top, axis=1, keepdims=True)
            total = None
            acc = None
            for d in range(window):
                place = pl.ds((last - d) * rows, rows)
                offset = row_top
                if d > 0:
                    offset = row_top + bias[which, d : d + 1, :1]
                weights = jnp.exp2((scores[d] - offset) * factor)
                for c in range(rows // DH):
                    lanes = weights[:, c * DH : (c + 1) * DH]
                    total = lanes if total is None else total + lanes
                product = jnp.dot(
                    weights.astype(jnp.bfloat16),
                    vbuf[g, place, :],
                    preferred_element_type=jnp.float32,
                )
                acc = product if acc is None else acc + product
            row_total = jnp.sum(total, axis=1, keepdims=True)
            obuf[:, cols] = (acc / row_total).astype(obuf.dtype)

        @pl.when(g < moved)
        def _():
            out_copy(step).start()

        @pl.when(g == moved)
        def _():
            out_local(step).start()

    for copy in moved_copies():
        copy.wait_send()

    @pl.loop(0, HK)
    def _(g):
        for d in range(1, window):

            @pl.when(ctx + d < n_ctx)
            def _():
                for copy in gather_copies(g, d):
                    copy.wait_send()

    @pl.loop(sent_steps, steps)
    def _(step):
        out_local(step).wait()

    @pl.loop(0, sent_steps)
    def _(step):
        out_copy(step).wait_send()
        out_copy(step).wait_recv()


def shards(n_pipe, n_ctx, queries, keys, values, doc_ids):
    rows = queries.shape[1]
    window = n_ctx // 2 + 1
    steps = HQ // STEP_HEADS
    bias_rows = (window + 7) // 8 * 8
    dma = pltpu.SemaphoreType.DMA
    anywhere = pl.BlockSpec(memory_space=pl.ANY)
    handed = pl.pallas_call(
        functools.partial(kernel, n_pipe, n_ctx, window, rows),
        out_shape=jax.ShapeDtypeStruct((rows, HQ * DH), jnp.bfloat16),
        in_specs=[pl.BlockSpec(memory_space=pltpu.SMEM), anywhere, anywhere, anywhere],
        out_specs=anywhere,
        scratch_shapes=[
            pltpu.VMEM((rows, HQ * DH), jnp.bfloat16),
            pltpu.VMEM((HK, window * rows, DH), jnp.bfloat16),
            pltpu.VMEM((HK, window * rows, DH), jnp.bfloat16),
            pltpu.VMEM((rows, HQ * DH), jnp.bfloat16),
            pltpu.VMEM((2, bias_rows, DH), jnp.float32),
            dma((HK,)),
            dma((2, HK)),
            dma((2, HK, window - 1)),
            dma((2, HK, window - 1)),
            dma((4,)),
            dma((4,)),
            dma((steps,)),
            dma((steps,)),
        ],
        compiler_params=pltpu.CompilerParams(
            collective_id=0, has_side_effects=True, vmem_limit_bytes=48 * 1024 * 1024
        ),
        name="relay_attention",
    )(doc_ids, queries[0], keys[0], values[0])
    return handed[None]


def solution(mesh):
    placed = (
        P("pipe", "ctx", None),
        P("pipe", "ctx", None),
        P("pipe", "ctx", None),
        P("pipe", None),
    )
    return jax.shard_map(
        functools.partial(shards, mesh.shape["pipe"], mesh.shape["ctx"]),
        mesh=mesh,
        in_specs=placed,
        out_specs=P("pipe", "ctx", None),
        check_vma=False,
    )
```

```python
import functools
import math

import jax
import jax.numpy as jnp
from jax import lax
from jax.experimental import pallas as pl
from jax.experimental.pallas import tpu as pltpu
from jax.sharding import PartitionSpec as P

HQ = 32
HK = 4
DH = 128
PER_GROUP = HQ // HK
STEP_HEADS = 2
HIDDEN = 1e30
MESH = pl.DeviceIdType.MESH


def kernel(
    n_pipe,
    n_ctx,
    window,
    rows,
    doc_hbm,
    q_ref,
    k_ref,
    v_ref,
    out_ref,
    qbuf,
    kbuf,
    vbuf,
    obuf,
    bias,
    doc_ref,
    doc_sem,
    q_sem,
    own_sem,
    kv_send,
    kv_recv,
    z_send,
    z_recv,
    o_send,
    o_recv,
):
    pipe = lax.axis_index("pipe")
    ctx = lax.axis_index("ctx")
    right = lax.rem(pipe + 1, n_pipe)
    left = lax.rem(pipe + n_pipe - 1, n_pipe)
    moved = HK - 1
    group_cols = PER_GROUP * DH
    step_cols = STEP_HEADS * DH
    steps = HQ // STEP_HEADS
    group_steps = PER_GROUP // STEP_HEADS
    sent_steps = moved * group_steps
    last = window - 1

    barrier = pltpu.get_barrier_semaphore()
    pl.semaphore_signal(barrier, inc=1, device_id=(left, ctx), device_id_type=MESH)
    pl.semaphore_signal(barrier, inc=1, device_id=(right, ctx), device_id_type=MESH)
    sibling_core = ctx + 1 - 2 * lax.rem(ctx, 2)
    pl.semaphore_signal(barrier, inc=1, device_id=(pipe, sibling_core), device_id_type=MESH)
    for d in range(2, window, 2):

        @pl.when(ctx >= d)
        def _():
            pl.semaphore_signal(barrier, inc=1, device_id=(pipe, ctx - d), device_id_type=MESH)

        @pl.when(ctx + d < n_ctx)
        def _():
            pl.semaphore_signal(barrier, inc=1, device_id=(pipe, ctx + d), device_id_type=MESH)

    def own_copies(g):
        cols = pl.ds(pl.multiple_of(g * DH, DH), DH)
        place = pl.ds(last * rows, rows)
        return (
            pltpu.make_async_copy(k_ref.at[:, cols], kbuf.at[g, place], own_sem.at[0, g]),
            pltpu.make_async_copy(v_ref.at[:, cols], vbuf.at[g, place], own_sem.at[1, g]),
        )

    def q_copy(g):
        cols = pl.ds(pl.multiple_of(g * group_cols, group_cols), group_cols)
        return pltpu.make_async_copy(q_ref.at[:, cols], qbuf.at[:, cols], q_sem.at[g])

    def kv_copies(g, source, target, ctx_to):
        from_rows = pl.ds(pl.multiple_of((last - source) * rows, rows), rows)
        to_rows = pl.ds(pl.multiple_of((last - target) * rows, rows), rows)
        return [
            pltpu.make_async_remote_copy(
                src_ref=buf.at[g, from_rows],
                dst_ref=buf.at[g, to_rows],
                send_sem=kv_send.at[which, g, target - 1],
                recv_sem=kv_recv.at[which, g, target - 1],
                device_id=(pipe, ctx_to),
                device_id_type=MESH,
            )
            for which, buf in ((0, kbuf), (1, vbuf))
        ]

    def direct(g, d):
        return kv_copies(g, 0, d, lax.rem(ctx + d, n_ctx))

    core = lax.rem(ctx, 2)
    turn = 1 - 2 * core
    sibling = ctx + turn

    def relay(g, d):
        return kv_copies(g, d, d + turn, sibling)

    def for_direct(do):
        for d in range(2, window, 2):
            pl.when(ctx + d < n_ctx)(functools.partial(do, d))

    def for_relay(do):
        for d in range(0, window, 2):
            if d == 0:
                fits = core == 0
            elif d == last:
                fits = (core == 1) & (ctx >= d)
            else:
                fits = ctx >= d
            pl.when(fits)(functools.partial(do, d))

    def start_all(make, g, d):
        for copy in make(g, d):
            copy.start()

    def end_send(make, g, d):
        for copy in make(g, d):
            copy.wait_send()

    def wait_block(g, d):
        for copy in kv_copies(g, 0, d, sibling):
            copy.wait_recv()

    def to_right(source, target, at):
        return pltpu.make_async_remote_copy(
            src_ref=source,
            dst_ref=target,
            send_sem=z_send.at[at],
            recv_sem=z_recv.at[at],
            device_id=(right, ctx),
            device_id_type=MESH,
        )

    def moved_copies():
        cols = pl.ds(moved * DH, DH)
        q_cols = pl.ds(moved * group_cols, group_cols)
        place = pl.ds(last * rows, rows)
        return (
            to_right(k_ref.at[:, cols], kbuf.at[moved, place], 0),
            to_right(v_ref.at[:, cols], vbuf.at[moved, place], 1),
            to_right(bias.at[0], bias.at[1], 2),
            to_right(q_ref.at[:, q_cols], qbuf.at[:, q_cols], 3),
        )

    def out_copy(step):
        cols = pl.ds(pl.multiple_of(step * step_cols, step_cols), step_cols)
        return pltpu.make_async_remote_copy(
            src_ref=obuf.at[:, cols],
            dst_ref=out_ref.at[:, cols],
            send_sem=o_send.at[step],
            recv_sem=o_recv.at[step],
            device_id=(right, ctx),
            device_id_type=MESH,
        )

    def out_local(step):
        cols = pl.ds(pl.multiple_of(step * step_cols, step_cols), step_cols)
        return pltpu.make_async_copy(obuf.at[:, cols], out_ref.at[:, cols], o_send.at[step])

    doc_copy = pltpu.make_async_copy(doc_hbm, doc_ref, doc_sem)
    doc_copy.start()
    for g in range(moved):
        for copy in own_copies(g):
            copy.start()
        q_copy(g).start()

    doc_copy.wait()
    bias[0] = jnp.zeros(bias.shape[1:], jnp.float32)
    own_doc = doc_ref[0, ctx]
    for d in range(window):
        block = jnp.maximum(ctx - d, 0)
        seen = (doc_ref[0, block] == own_doc) & (ctx >= d)
        bias[0, d : d + 1, :] = jnp.full((1, DH), jnp.where(seen, 0.0, HIDDEN), jnp.float32)

    for d in range(1, window):

        @pl.when(ctx < d)
        def _():
            place = pl.ds((last - d) * rows, rows)
            for g in range(HK):
                kbuf[g, place, :] = jnp.zeros((rows, DH), kbuf.dtype)
                vbuf[g, place, :] = jnp.zeros((rows, DH), vbuf.dtype)

    met = 3
    for d in range(2, window, 2):
        met = met + jnp.where(ctx >= d, 1, 0) + jnp.where(ctx + d < n_ctx, 1, 0)
    pl.semaphore_wait(barrier, met)

    for copy in moved_copies():
        copy.start()

    def start_direct(g):
        @pl.when(g < moved)
        def _():
            for copy in own_copies(g):
                copy.wait()

        @pl.when(g == moved)
        def _():
            for copy in moved_copies()[:3]:
                copy.wait_recv()

        for_direct(lambda d: start_all(direct, g, d))

    def start_relay(g):
        for d in range(2, window, 2):
            pl.when(ctx >= d)(functools.partial(wait_block, g, d))
        for_relay(lambda d: start_all(relay, g, d))

    def end_gather(g):
        for d in range(1, window, 2):
            pl.when(ctx >= d)(functools.partial(wait_block, g, d))

    start_direct(0)
    start_direct(1)
    start_relay(0)
    factor = math.log2(math.e) / math.sqrt(DH)

    @pl.loop(0, steps)
    def _(step):
        g = step // group_steps

        @pl.when(lax.rem(step, group_steps) == 0)
        def _():
            @pl.when(g < moved)
            def _():
                q_copy(g).wait()

            @pl.when(g == moved)
            def _():
                moved_copies()[3].wait_recv()

            end_gather(g)

            @pl.when(g + 1 < moved)
            def _():
                start_direct(g + 2)

        @pl.when((lax.rem(step, group_steps) == group_steps // 2) & (g < moved))
        def _():
            start_relay(g + 1)

        which = jnp.where(g == moved, 1, 0)
        causal = lax.broadcasted_iota(jnp.int32, (rows, rows), 0) >= lax.broadcasted_iota(
            jnp.int32, (rows, rows), 1
        )
        for at in range(STEP_HEADS):
            cols = pl.ds(pl.multiple_of(step * step_cols + at * DH, DH), DH)
            query = qbuf[:, cols]
            scores = []
            top = None
            for d in range(window):
                place = pl.ds((last - d) * rows, rows)
                part = lax.dot_general(
                    query,
                    kbuf[g, place, :],
                    (((1,), (1,)), ((), ())),
                    preferred_element_type=jnp.float32,
                )
                if d == 0:
                    part = jnp.where(causal, part, -HIDDEN)
                scores.append(part)
                lanes = part[:, :DH]
                for c in range(1, rows // DH):
                    lanes = jnp.maximum(lanes, part[:, c * DH : (c + 1) * DH])
                if d > 0:
                    lanes = lanes - bias[which, d : d + 1, :]
                top = lanes if top is None else jnp.maximum(top, lanes)
            row_top = jnp.max(top, axis=1, keepdims=True)
            total = None
            acc = None
            for d in range(window):
                place = pl.ds((last - d) * rows, rows)
                offset = row_top
                if d > 0:
                    offset = row_top + bias[which, d : d + 1, :1]
                weights = jnp.exp2((scores[d] - offset) * factor)
                for c in range(rows // DH):
                    lanes = weights[:, c * DH : (c + 1) * DH]
                    total = lanes if total is None else total + lanes
                product = jnp.dot(
                    weights.astype(jnp.bfloat16),
                    vbuf[g, place, :],
                    preferred_element_type=jnp.float32,
                )
                acc = product if acc is None else acc + product
            row_total = jnp.sum(total, axis=1, keepdims=True)
            obuf[:, cols] = (acc / row_total).astype(obuf.dtype)

        @pl.when(g < moved)
        def _():
            out_copy(step).start()

        @pl.when(g == moved)
        def _():
            out_local(step).start()

    for copy in moved_copies():
        copy.wait_send()

    @pl.loop(0, HK)
    def _(g):
        for_direct(lambda d: end_send(direct, g, d))
        for_relay(lambda d: end_send(relay, g, d))

    @pl.loop(sent_steps, steps)
    def _(step):
        out_local(step).wait()

    @pl.loop(0, sent_steps)
    def _(step):
        out_copy(step).wait_send()
        out_copy(step).wait_recv()


def shards(n_pipe, n_ctx, queries, keys, values, doc_ids):
    rows = queries.shape[1]
    window = n_ctx // 2 + 1
    steps = HQ // STEP_HEADS
    bias_rows = (window + 7) // 8 * 8
    dma = pltpu.SemaphoreType.DMA
    anywhere = pl.BlockSpec(memory_space=pl.ANY)
    handed = pl.pallas_call(
        functools.partial(kernel, n_pipe, n_ctx, window, rows),
        out_shape=jax.ShapeDtypeStruct((rows, HQ * DH), jnp.bfloat16),
        in_specs=[pl.BlockSpec(memory_space=pltpu.HBM)] * 4,
        out_specs=anywhere,
        scratch_shapes=[
            pltpu.VMEM((rows, HQ * DH), jnp.bfloat16),
            pltpu.VMEM((HK, window * rows, DH), jnp.bfloat16),
            pltpu.VMEM((HK, window * rows, DH), jnp.bfloat16),
            pltpu.VMEM((rows, HQ * DH), jnp.bfloat16),
            pltpu.VMEM((2, bias_rows, DH), jnp.float32),
            pltpu.SMEM(doc_ids.shape, jnp.int32),
            dma,
            dma((HK,)),
            dma((2, HK)),
            dma((2, HK, window - 1)),
            dma((2, HK, window - 1)),
            dma((4,)),
            dma((4,)),
            dma((steps,)),
            dma((steps,)),
        ],
        compiler_params=pltpu.CompilerParams(
            collective_id=0, has_side_effects=True, vmem_limit_bytes=48 * 1024 * 1024
        ),
        name="relay_attention",
    )(*(pltpu.with_memory_space_constraint(x, pltpu.HBM) for x in (doc_ids, queries[0], keys[0], values[0])))
    return handed[None]


def solution(mesh):
    placed = (
        P("pipe", "ctx", None),
        P("pipe", "ctx", None),
        P("pipe", "ctx", None),
        P("pipe", None),
    )
    return jax.shard_map(
        functools.partial(shards, mesh.shape["pipe"], mesh.shape["ctx"]),
        mesh=mesh,
        in_specs=placed,
        out_specs=P("pipe", "ctx", None),
        check_vma=False,
    )
```

```python
import functools
import math

import jax
import jax.numpy as jnp
from jax import lax
from jax.experimental import pallas as pl
from jax.experimental.pallas import tpu as pltpu
from jax.sharding import PartitionSpec as P

HQ = 32
HK = 4
DH = 128
PER_GROUP = HQ // HK
STEP_HEADS = 2
HIDDEN = 1e30
MESH = pl.DeviceIdType.MESH


def kernel(
    n_pipe,
    n_ctx,
    window,
    rows,
    doc_hbm,
    q_ref,
    k_ref,
    v_ref,
    out_ref,
    qbuf,
    kbuf,
    vbuf,
    obuf,
    bias,
    doc_ref,
    doc_sem,
    q_sem,
    own_sem,
    kv_send,
    kv_recv,
    z_send,
    z_recv,
    o_send,
    o_recv,
):
    pipe = lax.axis_index("pipe")
    ctx = lax.axis_index("ctx")
    right = lax.rem(pipe + 1, n_pipe)
    left = lax.rem(pipe + n_pipe - 1, n_pipe)
    moved = HK - 1
    group_cols = PER_GROUP * DH
    step_cols = STEP_HEADS * DH
    steps = HQ // STEP_HEADS
    group_steps = PER_GROUP // STEP_HEADS
    sent_steps = moved * group_steps
    last = window - 1

    barrier = pltpu.get_barrier_semaphore()
    pl.semaphore_signal(barrier, inc=1, device_id=(left, ctx), device_id_type=MESH)
    pl.semaphore_signal(barrier, inc=1, device_id=(right, ctx), device_id_type=MESH)
    sibling_core = ctx + 1 - 2 * lax.rem(ctx, 2)
    pl.semaphore_signal(barrier, inc=1, device_id=(pipe, sibling_core), device_id_type=MESH)
    for d in range(2, window, 2):

        @pl.when(ctx >= d)
        def _():
            pl.semaphore_signal(barrier, inc=1, device_id=(pipe, ctx - d), device_id_type=MESH)

        @pl.when(ctx + d < n_ctx)
        def _():
            pl.semaphore_signal(barrier, inc=1, device_id=(pipe, ctx + d), device_id_type=MESH)

    def own_copies(g):
        cols = pl.ds(pl.multiple_of(g * DH, DH), DH)
        place = pl.ds(last * rows, rows)
        return (
            pltpu.make_async_copy(k_ref.at[:, cols], kbuf.at[g, place], own_sem.at[0, g]),
            pltpu.make_async_copy(v_ref.at[:, cols], vbuf.at[g, place], own_sem.at[1, g]),
        )

    def q_copy(g):
        cols = pl.ds(pl.multiple_of(g * group_cols, group_cols), group_cols)
        return pltpu.make_async_copy(q_ref.at[:, cols], qbuf.at[:, cols], q_sem.at[g])

    def kv_copies(g, source, target, ctx_to):
        from_rows = pl.ds(pl.multiple_of((last - source) * rows, rows), rows)
        to_rows = pl.ds(pl.multiple_of((last - target) * rows, rows), rows)
        return [
            pltpu.make_async_remote_copy(
                src_ref=buf.at[g, from_rows],
                dst_ref=buf.at[g, to_rows],
                send_sem=kv_send.at[which, g, target - 1],
                recv_sem=kv_recv.at[which, g, target - 1],
                device_id=(pipe, ctx_to),
                device_id_type=MESH,
            )
            for which, buf in ((0, kbuf), (1, vbuf))
        ]

    def direct(g, d):
        return kv_copies(g, 0, d, lax.rem(ctx + d, n_ctx))

    core = lax.rem(ctx, 2)
    turn = 1 - 2 * core
    sibling = ctx + turn

    def relay(g, d):
        return kv_copies(g, d, d + turn, sibling)

    odd_chip = lax.rem(ctx // 2, 2) == 1
    even_chip = lax.rem(ctx // 2, 2) == 0

    def forward(g, d):
        return kv_copies(g, d, d - 2, lax.rem(ctx + n_ctx - 2, n_ctx))

    def for_direct(do):
        for d in range(2, window, 2):
            fits = even_chip if d == 2 else ctx + d < n_ctx
            pl.when(fits)(functools.partial(do, d))

    def for_forward(do):
        pl.when(odd_chip & (ctx >= 4))(functools.partial(do, 4))

    def for_relay(do, late):
        for d in range(0, window, 2):
            if late and d != 2:
                continue
            if d == 0:
                fits = core == 0
            elif d == 2:
                fits = (even_chip if late else odd_chip) & (ctx >= d)
            else:
                fits = ctx >= d
            if d == last:
                fits = fits & (core == 1)
            pl.when(fits)(functools.partial(do, d))

    def start_all(make, g, d):
        for copy in make(g, d):
            copy.start()

    def end_send(make, g, d):
        for copy in make(g, d):
            copy.wait_send()

    def wait_block(g, d):
        for copy in kv_copies(g, 0, d, sibling):
            copy.wait_recv()

    def to_right(source, target, at):
        return pltpu.make_async_remote_copy(
            src_ref=source,
            dst_ref=target,
            send_sem=z_send.at[at],
            recv_sem=z_recv.at[at],
            device_id=(right, ctx),
            device_id_type=MESH,
        )

    def moved_copies():
        cols = pl.ds(moved * DH, DH)
        q_cols = pl.ds(moved * group_cols, group_cols)
        place = pl.ds(last * rows, rows)
        return (
            to_right(k_ref.at[:, cols], kbuf.at[moved, place], 0),
            to_right(v_ref.at[:, cols], vbuf.at[moved, place], 1),
            to_right(bias.at[0], bias.at[1], 2),
            to_right(q_ref.at[:, q_cols], qbuf.at[:, q_cols], 3),
        )

    def out_copy(step):
        cols = pl.ds(pl.multiple_of(step * step_cols, step_cols), step_cols)
        return pltpu.make_async_remote_copy(
            src_ref=obuf.at[:, cols],
            dst_ref=out_ref.at[:, cols],
            send_sem=o_send.at[step],
            recv_sem=o_recv.at[step],
            device_id=(right, ctx),
            device_id_type=MESH,
        )

    def out_local(step):
        cols = pl.ds(pl.multiple_of(step * step_cols, step_cols), step_cols)
        return pltpu.make_async_copy(obuf.at[:, cols], out_ref.at[:, cols], o_send.at[step])

    doc_copy = pltpu.make_async_copy(doc_hbm, doc_ref, doc_sem)
    doc_copy.start()
    for g in range(moved):
        for copy in own_copies(g):
            copy.start()
        q_copy(g).start()

    doc_copy.wait()
    bias[0] = jnp.zeros(bias.shape[1:], jnp.float32)
    own_doc = doc_ref[0, ctx]
    for d in range(window):
        block = jnp.maximum(ctx - d, 0)
        seen = (doc_ref[0, block] == own_doc) & (ctx >= d)
        bias[0, d : d + 1, :] = jnp.full((1, DH), jnp.where(seen, 0.0, HIDDEN), jnp.float32)

    for d in range(1, window):

        @pl.when(ctx < d)
        def _():
            place = pl.ds((last - d) * rows, rows)
            for g in range(HK):
                kbuf[g, place, :] = jnp.zeros((rows, DH), kbuf.dtype)
                vbuf[g, place, :] = jnp.zeros((rows, DH), vbuf.dtype)

    met = 3
    for d in range(2, window, 2):
        met = met + jnp.where(ctx >= d, 1, 0) + jnp.where(ctx + d < n_ctx, 1, 0)
    pl.semaphore_wait(barrier, met)

    for copy in moved_copies():
        copy.start()

    def start_direct(g):
        if g < moved:
            for copy in own_copies(g):
                copy.wait()
        else:
            for copy in moved_copies()[:3]:
                copy.wait_recv()
        for_direct(lambda d: start_all(direct, g, d))

    def pass_on(g):
        for d in range(2, window, 2):
            fits = odd_chip if d == 2 else ctx >= d
            pl.when(fits)(functools.partial(wait_block, g, d))
        for_forward(lambda d: start_all(forward, g, d))
        for_relay(lambda d: start_all(relay, g, d), False)

    def pass_late(g):
        pl.when(even_chip & (ctx >= 2))(functools.partial(wait_block, g, 2))
        for_relay(lambda d: start_all(relay, g, d), True)

    def end_gather(g):
        for d in range(1, window, 2):
            pl.when(ctx >= d)(functools.partial(wait_block, g, d))

    start_direct(0)
    pass_on(0)
    start_direct(1)
    pass_late(0)
    pass_on(1)
    start_direct(2)
    factor = math.log2(math.e) / math.sqrt(DH)

    @pl.loop(0, steps)
    def _(step):
        g = step // group_steps

        @pl.when(lax.rem(step, group_steps) == 0)
        def _():
            @pl.when(g < moved)
            def _():
                q_copy(g).wait()

            @pl.when(g == moved)
            def _():
                moved_copies()[3].wait_recv()

            end_gather(g)

        @pl.when(step == 1)
        def _():
            pass_late(1)
            pass_on(2)
            start_direct(3)

        @pl.when(step == 3)
        def _():
            pass_late(2)
            pass_on(3)

        @pl.when(step == 5)
        def _():
            pass_late(3)

        which = jnp.where(g == moved, 1, 0)
        causal = lax.broadcasted_iota(jnp.int32, (rows, rows), 0) >= lax.broadcasted_iota(
            jnp.int32, (rows, rows), 1
        )
        for at in range(STEP_HEADS):
            cols = pl.ds(pl.multiple_of(step * step_cols + at * DH, DH), DH)
            query = qbuf[:, cols]
            scores = []
            top = None
            for d in range(window):
                place = pl.ds((last - d) * rows, rows)
                part = lax.dot_general(
                    query,
                    kbuf[g, place, :],
                    (((1,), (1,)), ((), ())),
                    preferred_element_type=jnp.float32,
                )
                if d == 0:
                    part = jnp.where(causal, part, -HIDDEN)
                scores.append(part)
                lanes = part[:, :DH]
                for c in range(1, rows // DH):
                    lanes = jnp.maximum(lanes, part[:, c * DH : (c + 1) * DH])
                if d > 0:
                    lanes = lanes - bias[which, d : d + 1, :]
                top = lanes if top is None else jnp.maximum(top, lanes)
            row_top = jnp.broadcast_to(jnp.max(top, axis=1, keepdims=True), (rows, DH))
            total = None
            acc = None
            for d in range(window):
                place = pl.ds((last - d) * rows, rows)
                offset = row_top
                if d > 0:
                    offset = row_top + bias[which, d : d + 1, :]
                rounded = []
                for c in range(rows // DH):
                    lanes = jnp.exp2((scores[d][:, c * DH : (c + 1) * DH] - offset) * factor)
                    total = lanes if total is None else total + lanes
                    rounded.append(lanes.astype(jnp.bfloat16))
                product = jnp.dot(
                    jnp.concatenate(rounded, axis=1),
                    vbuf[g, place, :],
                    preferred_element_type=jnp.float32,
                )
                acc = product if acc is None else acc + product
            row_total = jnp.sum(total, axis=1, keepdims=True)
            obuf[:, cols] = (acc / row_total).astype(obuf.dtype)

        @pl.when(g < moved)
        def _():
            out_copy(step).start()

        @pl.when(g == moved)
        def _():
            out_local(step).start()

    for copy in moved_copies():
        copy.wait_send()

    @pl.loop(0, HK)
    def _(g):
        for_direct(lambda d: end_send(direct, g, d))
        for_forward(lambda d: end_send(forward, g, d))
        for_relay(lambda d: end_send(relay, g, d), False)
        for_relay(lambda d: end_send(relay, g, d), True)

    @pl.loop(sent_steps, steps)
    def _(step):
        out_local(step).wait()

    @pl.loop(0, sent_steps)
    def _(step):
        out_copy(step).wait_send()
        out_copy(step).wait_recv()


def shards(n_pipe, n_ctx, queries, keys, values, doc_ids):
    rows = queries.shape[1]
    window = n_ctx // 2 + 1
    steps = HQ // STEP_HEADS
    bias_rows = (window + 7) // 8 * 8
    dma = pltpu.SemaphoreType.DMA
    anywhere = pl.BlockSpec(memory_space=pl.ANY)
    handed = pl.pallas_call(
        functools.partial(kernel, n_pipe, n_ctx, window, rows),
        out_shape=jax.ShapeDtypeStruct((rows, HQ * DH), jnp.bfloat16),
        in_specs=[pl.BlockSpec(memory_space=pltpu.HBM)] * 4,
        out_specs=anywhere,
        scratch_shapes=[
            pltpu.VMEM((rows, HQ * DH), jnp.bfloat16),
            pltpu.VMEM((HK, window * rows, DH), jnp.bfloat16),
            pltpu.VMEM((HK, window * rows, DH), jnp.bfloat16),
            pltpu.VMEM((rows, HQ * DH), jnp.bfloat16),
            pltpu.VMEM((2, bias_rows, DH), jnp.float32),
            pltpu.SMEM(doc_ids.shape, jnp.int32),
            dma,
            dma((HK,)),
            dma((2, HK)),
            dma((2, HK, window - 1)),
            dma((2, HK, window - 1)),
            dma((4,)),
            dma((4,)),
            dma((steps,)),
            dma((steps,)),
        ],
        compiler_params=pltpu.CompilerParams(
            collective_id=0, has_side_effects=True, vmem_limit_bytes=48 * 1024 * 1024
        ),
        name="relay_attention",
    )(*(pltpu.with_memory_space_constraint(x, pltpu.HBM) for x in (doc_ids, queries[0], keys[0], values[0])))
    return handed[None]


def solution(mesh):
    placed = (
        P("pipe", "ctx", None),
        P("pipe", "ctx", None),
        P("pipe", "ctx", None),
        P("pipe", None),
    )
    return jax.shard_map(
        functools.partial(shards, mesh.shape["pipe"], mesh.shape["ctx"]),
        mesh=mesh,
        in_specs=placed,
        out_specs=P("pipe", "ctx", None),
        check_vma=False,
    )
```

```python
import functools
import math

import jax
import jax.numpy as jnp
from jax import lax
from jax.experimental import pallas as pl
from jax.experimental.pallas import tpu as pltpu
from jax.sharding import PartitionSpec as P

HQ = 32
HK = 4
DH = 128
PER_GROUP = HQ // HK
STEP_HEADS = 2
HIDDEN = 1e30
MESH = pl.DeviceIdType.MESH


def kernel(
    n_pipe,
    n_ctx,
    window,
    rows,
    doc_hbm,
    q_ref,
    k_ref,
    v_ref,
    out_ref,
    qbuf,
    kbuf,
    vbuf,
    obuf,
    bias,
    doc_ref,
    doc_sem,
    q_sem,
    own_sem,
    kv_send,
    kv_recv,
    z_send,
    z_recv,
    o_send,
    o_recv,
):
    pipe = lax.axis_index("pipe")
    ctx = lax.axis_index("ctx")
    right = lax.rem(pipe + 1, n_pipe)
    left = lax.rem(pipe + n_pipe - 1, n_pipe)
    moved = HK - 1
    group_cols = PER_GROUP * DH
    step_cols = STEP_HEADS * DH
    steps = HQ // STEP_HEADS
    group_steps = PER_GROUP // STEP_HEADS
    sent_steps = moved * group_steps
    last = window - 1

    core = lax.rem(ctx, 2)
    odd_chip = lax.rem(ctx // 2, 2) == 1
    even_chip = lax.rem(ctx // 2, 2) == 0
    turn = 1 - 2 * core
    sibling = ctx + turn
    barrier = pltpu.get_barrier_semaphore()

    def greet(pipe_to, ctx_to):
        pl.semaphore_signal(barrier, inc=1, device_id=(pipe_to, ctx_to), device_id_type=MESH)

    greet(left, ctx)
    pl.when((core == 1) | (ctx >= 2))(lambda: greet(pipe, sibling))
    pl.when(odd_chip)(lambda: greet(pipe, lax.rem(ctx + n_ctx - 2, n_ctx)))
    pl.when(even_chip & (ctx >= 2))(lambda: greet(pipe, lax.rem(ctx + 2, n_ctx)))
    met = 1 + jnp.where((core == 0) | (ctx >= 2), 1, 0)
    met = met + jnp.where(even_chip, 1, 0) + jnp.where(odd_chip & (ctx >= 4), 1, 0)
    for d in range(4, window, 2):
        pl.when(ctx >= d)(lambda d=d: greet(pipe, lax.rem(ctx + n_ctx - d, n_ctx)))
        met = met + jnp.where(ctx + d < n_ctx, 1, 0)

    def own_copies(g):
        cols = pl.ds(pl.multiple_of(g * DH, DH), DH)
        place = pl.ds(last * rows, rows)
        return (
            pltpu.make_async_copy(k_ref.at[:, cols], kbuf.at[g, place], own_sem.at[0, g]),
            pltpu.make_async_copy(v_ref.at[:, cols], vbuf.at[g, place], own_sem.at[1, g]),
        )

    def q_copy(g):
        cols = pl.ds(pl.multiple_of(g * group_cols, group_cols), group_cols)
        return pltpu.make_async_copy(q_ref.at[:, cols], qbuf.at[:, cols], q_sem.at[g])

    def kv_copies(g, source, target, ctx_to):
        from_rows = pl.ds(pl.multiple_of((last - source) * rows, rows), rows)
        to_rows = pl.ds(pl.multiple_of((last - target) * rows, rows), rows)
        return [
            pltpu.make_async_remote_copy(
                src_ref=buf.at[g, from_rows],
                dst_ref=buf.at[g, to_rows],
                send_sem=kv_send.at[which, g, target - 1],
                recv_sem=kv_recv.at[which, g, target - 1],
                device_id=(pipe, ctx_to),
                device_id_type=MESH,
            )
            for which, buf in ((0, kbuf), (1, vbuf))
        ]

    def direct(g, d):
        return kv_copies(g, 0, d, lax.rem(ctx + d, n_ctx))

    def relay(g, d):
        return kv_copies(g, d, d + turn, sibling)

    def forward(g, d):
        return kv_copies(g, d, d - 2, lax.rem(ctx + n_ctx - 2, n_ctx))

    def for_direct(do):
        for d in range(2, window, 2):
            fits = even_chip if d == 2 else ctx + d < n_ctx
            pl.when(fits)(functools.partial(do, d))

    def for_forward(do):
        pl.when(odd_chip & (ctx >= 4))(functools.partial(do, 4))

    def for_relay(do, late):
        for d in range(0, window, 2):
            if late and d != 2:
                continue
            if d == 0:
                fits = core == 0
            elif d == 2:
                fits = (even_chip if late else odd_chip) & (ctx >= d)
            else:
                fits = ctx >= d
            if d == last:
                fits = fits & (core == 1)
            pl.when(fits)(functools.partial(do, d))

    def start_all(make, g, d):
        for copy in make(g, d):
            copy.start()

    def end_send(make, g, d):
        for copy in make(g, d):
            copy.wait_send()

    def wait_block(g, d):
        for copy in kv_copies(g, 0, d, sibling):
            copy.wait_recv()

    def to_right(source, target, at):
        return pltpu.make_async_remote_copy(
            src_ref=source,
            dst_ref=target,
            send_sem=z_send.at[at],
            recv_sem=z_recv.at[at],
            device_id=(right, ctx),
            device_id_type=MESH,
        )

    def moved_copies():
        cols = pl.ds(moved * DH, DH)
        q_cols = pl.ds(moved * group_cols, group_cols)
        place = pl.ds(last * rows, rows)
        return (
            to_right(k_ref.at[:, cols], kbuf.at[moved, place], 0),
            to_right(v_ref.at[:, cols], vbuf.at[moved, place], 1),
            to_right(bias.at[0], bias.at[1], 2),
            to_right(q_ref.at[:, q_cols], qbuf.at[:, q_cols], 3),
        )

    def out_copy(step):
        cols = pl.ds(pl.multiple_of(step * step_cols, step_cols), step_cols)
        return pltpu.make_async_remote_copy(
            src_ref=obuf.at[:, cols],
            dst_ref=out_ref.at[:, cols],
            send_sem=o_send.at[step],
            recv_sem=o_recv.at[step],
            device_id=(right, ctx),
            device_id_type=MESH,
        )

    def out_local(step):
        cols = pl.ds(pl.multiple_of(step * step_cols, step_cols), step_cols)
        return pltpu.make_async_copy(obuf.at[:, cols], out_ref.at[:, cols], o_send.at[step])

    doc_copy = pltpu.make_async_copy(doc_hbm, doc_ref, doc_sem)
    doc_copy.start()
    for g in range(moved):
        for copy in own_copies(g):
            copy.start()
        q_copy(g).start()

    pl.semaphore_wait(barrier, met)
    for at in (0, 1, 3):
        moved_copies()[at].start()

    doc_copy.wait()
    bias[0] = jnp.zeros(bias.shape[1:], jnp.float32)
    own_doc = doc_ref[0, ctx]
    for d in range(window):
        block = jnp.maximum(ctx - d, 0)
        seen = (doc_ref[0, block] == own_doc) & (ctx >= d)
        bias[0, d : d + 1, :] = jnp.full((1, DH), jnp.where(seen, 0.0, HIDDEN), jnp.float32)

    moved_copies()[2].start()

    def start_direct(g):
        if g < moved:
            for copy in own_copies(g):
                copy.wait()
        else:
            for copy in moved_copies()[:3]:
                copy.wait_recv()
        for_direct(lambda d: start_all(direct, g, d))

    def pass_on(g):
        for d in range(2, window, 2):
            fits = odd_chip if d == 2 else ctx >= d
            pl.when(fits)(functools.partial(wait_block, g, d))
        for_forward(lambda d: start_all(forward, g, d))
        for_relay(lambda d: start_all(relay, g, d), False)

    def pass_late(g):
        pl.when(even_chip & (ctx >= 2))(functools.partial(wait_block, g, 2))
        for_relay(lambda d: start_all(relay, g, d), True)

    def end_gather(g):
        for d in range(1, window, 2):
            pl.when(ctx >= d)(functools.partial(wait_block, g, d))

    start_direct(0)
    for d in range(1, window):

        @pl.when(ctx < d)
        def _():
            place = pl.ds((last - d) * rows, rows)
            for g in range(HK):
                kbuf[g, place, :] = jnp.zeros((rows, DH), kbuf.dtype)
                vbuf[g, place, :] = jnp.zeros((rows, DH), vbuf.dtype)

    pass_on(0)
    start_direct(1)
    pass_late(0)
    pass_on(1)
    start_direct(2)
    factor = math.log2(math.e) / math.sqrt(DH)

    @pl.loop(0, steps)
    def _(step):
        g = step // group_steps

        @pl.when(lax.rem(step, group_steps) == 0)
        def _():
            @pl.when(g < moved)
            def _():
                q_copy(g).wait()

            @pl.when(g == moved)
            def _():
                moved_copies()[3].wait_recv()

            end_gather(g)

        @pl.when(step == 1)
        def _():
            pass_late(1)
            pass_on(2)
            start_direct(3)

        @pl.when(step == 3)
        def _():
            pass_late(2)
            pass_on(3)

        @pl.when(step == 5)
        def _():
            pass_late(3)

        which = jnp.where(g == moved, 1, 0)
        causal = lax.broadcasted_iota(jnp.int32, (rows, rows), 0) >= lax.broadcasted_iota(
            jnp.int32, (rows, rows), 1
        )
        for at in range(STEP_HEADS):
            cols = pl.ds(pl.multiple_of(step * step_cols + at * DH, DH), DH)
            query = qbuf[:, cols]
            scores = []
            top = None
            for d in range(window):
                place = pl.ds((last - d) * rows, rows)
                part = lax.dot_general(
                    query,
                    kbuf[g, place, :],
                    (((1,), (1,)), ((), ())),
                    preferred_element_type=jnp.float32,
                )
                if d == 0:
                    part = jnp.where(causal, part, -HIDDEN)
                scores.append(part)
                lanes = part[:, :DH]
                for c in range(1, rows // DH):
                    lanes = jnp.maximum(lanes, part[:, c * DH : (c + 1) * DH])
                if d > 0:
                    lanes = lanes - bias[which, d : d + 1, :]
                top = lanes if top is None else jnp.maximum(top, lanes)
            row_top = jnp.broadcast_to(jnp.max(top, axis=1, keepdims=True), (rows, DH))
            total = None
            acc = None
            for d in range(window):
                place = pl.ds((last - d) * rows, rows)
                offset = row_top
                if d > 0:
                    offset = row_top + bias[which, d : d + 1, :]
                rounded = []
                for c in range(rows // DH):
                    lanes = jnp.exp2((scores[d][:, c * DH : (c + 1) * DH] - offset) * factor)
                    total = lanes if total is None else total + lanes
                    rounded.append(lanes.astype(jnp.bfloat16))
                product = jnp.dot(
                    jnp.concatenate(rounded, axis=1),
                    vbuf[g, place, :],
                    preferred_element_type=jnp.float32,
                )
                acc = product if acc is None else acc + product
            row_total = jnp.sum(total, axis=1, keepdims=True)
            obuf[:, cols] = (acc / row_total).astype(obuf.dtype)

        @pl.when(g < moved)
        def _():
            out_copy(step).start()

        @pl.when(g == moved)
        def _():
            out_local(step).start()

    for copy in moved_copies():
        copy.wait_send()

    @pl.loop(0, HK)
    def _(g):
        for_direct(lambda d: end_send(direct, g, d))
        for_forward(lambda d: end_send(forward, g, d))
        for_relay(lambda d: end_send(relay, g, d), False)
        for_relay(lambda d: end_send(relay, g, d), True)

    @pl.loop(sent_steps, steps)
    def _(step):
        out_local(step).wait()

    @pl.loop(0, sent_steps)
    def _(step):
        out_copy(step).wait_send()
        out_copy(step).wait_recv()


def shards(n_pipe, n_ctx, queries, keys, values, doc_ids):
    rows = queries.shape[1]
    window = n_ctx // 2 + 1
    steps = HQ // STEP_HEADS
    bias_rows = (window + 7) // 8 * 8
    dma = pltpu.SemaphoreType.DMA
    anywhere = pl.BlockSpec(memory_space=pl.ANY)
    handed = pl.pallas_call(
        functools.partial(kernel, n_pipe, n_ctx, window, rows),
        out_shape=jax.ShapeDtypeStruct((rows, HQ * DH), jnp.bfloat16),
        in_specs=[pl.BlockSpec(memory_space=pltpu.HBM)] * 4,
        out_specs=anywhere,
        scratch_shapes=[
            pltpu.VMEM((rows, HQ * DH), jnp.bfloat16),
            pltpu.VMEM((HK, window * rows, DH), jnp.bfloat16),
            pltpu.VMEM((HK, window * rows, DH), jnp.bfloat16),
            pltpu.VMEM((rows, HQ * DH), jnp.bfloat16),
            pltpu.VMEM((2, bias_rows, DH), jnp.float32),
            pltpu.SMEM(doc_ids.shape, jnp.int32),
            dma,
            dma((HK,)),
            dma((2, HK)),
            dma((2, HK, window - 1)),
            dma((2, HK, window - 1)),
            dma((4,)),
            dma((4,)),
            dma((steps,)),
            dma((steps,)),
        ],
        compiler_params=pltpu.CompilerParams(
            collective_id=0, has_side_effects=True, vmem_limit_bytes=48 * 1024 * 1024
        ),
        name="relay_attention",
    )(*(pltpu.with_memory_space_constraint(x, pltpu.HBM) for x in (doc_ids, queries[0], keys[0], values[0])))
    return handed[None]


def solution(mesh):
    placed = (
        P("pipe", "ctx", None),
        P("pipe", "ctx", None),
        P("pipe", "ctx", None),
        P("pipe", None),
    )
    return jax.shard_map(
        functools.partial(shards, mesh.shape["pipe"], mesh.shape["ctx"]),
        mesh=mesh,
        in_specs=placed,
        out_specs=P("pipe", "ctx", None),
        check_vma=False,
    )
```

```python
import functools
import math

import jax
import jax.numpy as jnp
from jax import lax
from jax.experimental import pallas as pl
from jax.experimental.pallas import tpu as pltpu
from jax.sharding import PartitionSpec as P

HQ = 32
HK = 4
DH = 128
PER_GROUP = HQ // HK
STEP_HEADS = 1
HIDDEN = 1e30
MESH = pl.DeviceIdType.MESH


def kernel(
    n_pipe,
    n_ctx,
    window,
    rows,
    doc_hbm,
    q_ref,
    k_ref,
    v_ref,
    out_ref,
    qbuf,
    kbuf,
    vbuf,
    obuf,
    bias,
    doc_ref,
    doc_sem,
    q_sem,
    own_sem,
    kv_send,
    kv_recv,
    z_send,
    z_recv,
    o_send,
    o_recv,
):
    pipe = lax.axis_index("pipe")
    ctx = lax.axis_index("ctx")
    right = lax.rem(pipe + 1, n_pipe)
    left = lax.rem(pipe + n_pipe - 1, n_pipe)
    moved = HK - 1
    group_cols = PER_GROUP * DH
    step_cols = STEP_HEADS * DH
    steps = HQ // STEP_HEADS
    group_steps = PER_GROUP // STEP_HEADS
    sent_steps = moved * group_steps
    last = window - 1

    core = lax.rem(ctx, 2)
    odd_chip = lax.rem(ctx // 2, 2) == 1
    even_chip = lax.rem(ctx // 2, 2) == 0
    turn = 1 - 2 * core
    sibling = ctx + turn
    barrier = pltpu.get_barrier_semaphore()

    def greet(pipe_to, ctx_to):
        pl.semaphore_signal(barrier, inc=1, device_id=(pipe_to, ctx_to), device_id_type=MESH)

    greet(left, ctx)
    pl.when((core == 1) | (ctx >= 2))(lambda: greet(pipe, sibling))
    pl.when(odd_chip)(lambda: greet(pipe, lax.rem(ctx + n_ctx - 2, n_ctx)))
    pl.when(even_chip & (ctx >= 2))(lambda: greet(pipe, lax.rem(ctx + 2, n_ctx)))
    met = 1 + jnp.where((core == 0) | (ctx >= 2), 1, 0)
    met = met + jnp.where(even_chip, 1, 0) + jnp.where(odd_chip & (ctx >= 4), 1, 0)
    for d in range(4, window, 2):
        pl.when(ctx >= d)(lambda d=d: greet(pipe, lax.rem(ctx + n_ctx - d, n_ctx)))
        met = met + jnp.where(ctx + d < n_ctx, 1, 0)

    def own_copies(g):
        cols = pl.ds(pl.multiple_of(g * DH, DH), DH)
        place = pl.ds(last * rows, rows)
        return (
            pltpu.make_async_copy(k_ref.at[:, cols], kbuf.at[g, place], own_sem.at[0, g]),
            pltpu.make_async_copy(v_ref.at[:, cols], vbuf.at[g, place], own_sem.at[1, g]),
        )

    def q_copy(g):
        cols = pl.ds(pl.multiple_of(g * group_cols, group_cols), group_cols)
        return pltpu.make_async_copy(q_ref.at[:, cols], qbuf.at[:, cols], q_sem.at[g])

    def kv_copies(g, source, target, ctx_to):
        from_rows = pl.ds(pl.multiple_of((last - source) * rows, rows), rows)
        to_rows = pl.ds(pl.multiple_of((last - target) * rows, rows), rows)
        return [
            pltpu.make_async_remote_copy(
                src_ref=buf.at[g, from_rows],
                dst_ref=buf.at[g, to_rows],
                send_sem=kv_send.at[which, g, target - 1],
                recv_sem=kv_recv.at[which, g, target - 1],
                device_id=(pipe, ctx_to),
                device_id_type=MESH,
            )
            for which, buf in ((0, kbuf), (1, vbuf))
        ]

    def direct(g, d):
        return kv_copies(g, 0, d, lax.rem(ctx + d, n_ctx))

    def relay(g, d):
        return kv_copies(g, d, d + turn, sibling)

    def forward(g, d):
        return kv_copies(g, d, d - 2, lax.rem(ctx + n_ctx - 2, n_ctx))

    def for_direct(do):
        for d in range(2, window, 2):
            fits = even_chip if d == 2 else ctx + d < n_ctx
            pl.when(fits)(functools.partial(do, d))

    def for_forward(do):
        pl.when(odd_chip & (ctx >= 4))(functools.partial(do, 4))

    def for_relay(do, late):
        for d in range(0, window, 2):
            if late and d != 2:
                continue
            if d == 0:
                fits = core == 0
            elif d == 2:
                fits = (even_chip if late else odd_chip) & (ctx >= d)
            else:
                fits = ctx >= d
            if d == last:
                fits = fits & (core == 1)
            pl.when(fits)(functools.partial(do, d))

    def start_all(make, g, d):
        for copy in make(g, d):
            copy.start()

    def end_send(make, g, d):
        for copy in make(g, d):
            copy.wait_send()

    def wait_block(g, d):
        for copy in kv_copies(g, 0, d, sibling):
            copy.wait_recv()

    def to_right(source, target, at):
        return pltpu.make_async_remote_copy(
            src_ref=source,
            dst_ref=target,
            send_sem=z_send.at[at],
            recv_sem=z_recv.at[at],
            device_id=(right, ctx),
            device_id_type=MESH,
        )

    def moved_copies():
        cols = pl.ds(moved * DH, DH)
        q_cols = pl.ds(moved * group_cols, group_cols)
        place = pl.ds(last * rows, rows)
        return (
            to_right(k_ref.at[:, cols], kbuf.at[moved, place], 0),
            to_right(v_ref.at[:, cols], vbuf.at[moved, place], 1),
            to_right(bias.at[0], bias.at[1], 2),
            to_right(q_ref.at[:, q_cols], qbuf.at[:, q_cols], 3),
        )

    def out_copy(step):
        cols = pl.ds(pl.multiple_of(step * step_cols, step_cols), step_cols)
        return pltpu.make_async_remote_copy(
            src_ref=obuf.at[:, cols],
            dst_ref=out_ref.at[:, cols],
            send_sem=o_send.at[step],
            recv_sem=o_recv.at[step],
            device_id=(right, ctx),
            device_id_type=MESH,
        )

    def out_local(step):
        cols = pl.ds(pl.multiple_of(step * step_cols, step_cols), step_cols)
        return pltpu.make_async_copy(obuf.at[:, cols], out_ref.at[:, cols], o_send.at[step])

    doc_copy = pltpu.make_async_copy(doc_hbm, doc_ref, doc_sem)
    doc_copy.start()
    for g in range(moved):
        for copy in own_copies(g):
            copy.start()
        q_copy(g).start()

    pl.semaphore_wait(barrier, met)
    for at in (0, 1, 3):
        moved_copies()[at].start()

    doc_copy.wait()
    bias[0] = jnp.zeros(bias.shape[1:], jnp.float32)
    own_doc = doc_ref[0, ctx]
    for d in range(window):
        block = jnp.maximum(ctx - d, 0)
        seen = (doc_ref[0, block] == own_doc) & (ctx >= d)
        bias[0, d : d + 1, :] = jnp.full((1, DH), jnp.where(seen, 0.0, HIDDEN), jnp.float32)

    moved_copies()[2].start()

    def start_direct(g):
        if g < moved:
            for copy in own_copies(g):
                copy.wait()
        else:
            for copy in moved_copies()[:3]:
                copy.wait_recv()
        for_direct(lambda d: start_all(direct, g, d))

    def pass_on(g):
        for d in range(2, window, 2):
            fits = odd_chip if d == 2 else ctx >= d
            pl.when(fits)(functools.partial(wait_block, g, d))
        for_forward(lambda d: start_all(forward, g, d))
        for_relay(lambda d: start_all(relay, g, d), False)

    def pass_late(g):
        pl.when(even_chip & (ctx >= 2))(functools.partial(wait_block, g, 2))
        for_relay(lambda d: start_all(relay, g, d), True)

    def end_gather(g):
        for d in range(1, window, 2):
            pl.when(ctx >= d)(functools.partial(wait_block, g, d))

    start_direct(0)
    for d in range(1, window):

        @pl.when(ctx < d)
        def _():
            place = pl.ds((last - d) * rows, rows)
            for g in range(HK):
                kbuf[g, place, :] = jnp.zeros((rows, DH), kbuf.dtype)
                vbuf[g, place, :] = jnp.zeros((rows, DH), vbuf.dtype)

    pass_on(0)
    start_direct(1)
    pass_late(0)
    pass_on(1)
    start_direct(2)
    factor = math.log2(math.e) / math.sqrt(DH)

    @pl.loop(0, steps)
    def _(step):
        g = step // group_steps

        @pl.when(lax.rem(step, group_steps) == 0)
        def _():
            @pl.when(g < moved)
            def _():
                q_copy(g).wait()

            @pl.when(g == moved)
            def _():
                moved_copies()[3].wait_recv()

            end_gather(g)

        @pl.when(step == 1)
        def _():
            pass_late(1)
            pass_on(2)
            start_direct(3)

        @pl.when(step == 3)
        def _():
            pass_late(2)
            pass_on(3)

        @pl.when(step == 5)
        def _():
            pass_late(3)

        which = jnp.where(g == moved, 1, 0)
        causal = lax.broadcasted_iota(jnp.int32, (rows, rows), 0) >= lax.broadcasted_iota(
            jnp.int32, (rows, rows), 1
        )
        for at in range(STEP_HEADS):
            cols = pl.ds(pl.multiple_of(step * step_cols + at * DH, DH), DH)
            query = qbuf[:, cols]
            scores = []
            top = None
            for d in range(window):
                place = pl.ds((last - d) * rows, rows)
                part = lax.dot_general(
                    query,
                    kbuf[g, place, :],
                    (((1,), (1,)), ((), ())),
                    preferred_element_type=jnp.float32,
                )
                if d == 0:
                    part = jnp.where(causal, part, -HIDDEN)
                scores.append(part)
                lanes = part[:, :DH]
                for c in range(1, rows // DH):
                    lanes = jnp.maximum(lanes, part[:, c * DH : (c + 1) * DH])
                if d > 0:
                    lanes = lanes - bias[which, d : d + 1, :]
                top = lanes if top is None else jnp.maximum(top, lanes)
            row_top = jnp.broadcast_to(jnp.max(top, axis=1, keepdims=True), (rows, DH))
            total = None
            acc = None
            for d in range(window):
                place = pl.ds((last - d) * rows, rows)
                offset = row_top
                if d > 0:
                    offset = row_top + bias[which, d : d + 1, :]
                rounded = []
                for c in range(rows // DH):
                    lanes = jnp.exp2((scores[d][:, c * DH : (c + 1) * DH] - offset) * factor)
                    total = lanes if total is None else total + lanes
                    rounded.append(lanes.astype(jnp.bfloat16))
                product = jnp.dot(
                    jnp.concatenate(rounded, axis=1),
                    vbuf[g, place, :],
                    preferred_element_type=jnp.float32,
                )
                acc = product if acc is None else acc + product
            row_total = jnp.sum(total, axis=1, keepdims=True)
            obuf[:, cols] = (acc / row_total).astype(obuf.dtype)

        @pl.when(g < moved)
        def _():
            out_copy(step).start()

        @pl.when(g == moved)
        def _():
            out_local(step).start()

    for copy in moved_copies():
        copy.wait_send()

    @pl.loop(0, HK)
    def _(g):
        for_direct(lambda d: end_send(direct, g, d))
        for_forward(lambda d: end_send(forward, g, d))
        for_relay(lambda d: end_send(relay, g, d), False)
        for_relay(lambda d: end_send(relay, g, d), True)

    @pl.loop(sent_steps, steps)
    def _(step):
        out_local(step).wait()

    @pl.loop(0, sent_steps)
    def _(step):
        out_copy(step).wait_send()
        out_copy(step).wait_recv()


def shards(n_pipe, n_ctx, queries, keys, values, doc_ids):
    rows = queries.shape[1]
    window = n_ctx // 2 + 1
    steps = HQ // STEP_HEADS
    bias_rows = (window + 7) // 8 * 8
    dma = pltpu.SemaphoreType.DMA
    anywhere = pl.BlockSpec(memory_space=pl.ANY)
    handed = pl.pallas_call(
        functools.partial(kernel, n_pipe, n_ctx, window, rows),
        out_shape=jax.ShapeDtypeStruct((rows, HQ * DH), jnp.bfloat16),
        in_specs=[pl.BlockSpec(memory_space=pltpu.HBM)] * 4,
        out_specs=anywhere,
        scratch_shapes=[
            pltpu.VMEM((rows, HQ * DH), jnp.bfloat16),
            pltpu.VMEM((HK, window * rows, DH), jnp.bfloat16),
            pltpu.VMEM((HK, window * rows, DH), jnp.bfloat16),
            pltpu.VMEM((rows, HQ * DH), jnp.bfloat16),
            pltpu.VMEM((2, bias_rows, DH), jnp.float32),
            pltpu.SMEM(doc_ids.shape, jnp.int32),
            dma,
            dma((HK,)),
            dma((2, HK)),
            dma((2, HK, window - 1)),
            dma((2, HK, window - 1)),
            dma((4,)),
            dma((4,)),
            dma((steps,)),
            dma((steps,)),
        ],
        compiler_params=pltpu.CompilerParams(
            collective_id=0, has_side_effects=True, vmem_limit_bytes=48 * 1024 * 1024
        ),
        name="relay_attention",
    )(*(pltpu.with_memory_space_constraint(x, pltpu.HBM) for x in (doc_ids, queries[0], keys[0], values[0])))
    return handed[None]


def solution(mesh):
    placed = (
        P("pipe", "ctx", None),
        P("pipe", "ctx", None),
        P("pipe", "ctx", None),
        P("pipe", None),
    )
    return jax.shard_map(
        functools.partial(shards, mesh.shape["pipe"], mesh.shape["ctx"]),
        mesh=mesh,
        in_specs=placed,
        out_specs=P("pipe", "ctx", None),
        check_vma=False,
    )
```
